128 devices in a mesh: gx: 8 (over y, z_hi), gy: 16 (over z_lo, x, core).
Axes of the slice: x: 4, y: 4, z: 4 (z_hi: 2, z_lo: 2; z = z_hi * 2 + z_lo), core: 2. Of those that a mesh axis runs over, the one named last changes fastest.
Arguments:
- saved_conc: float32 [3, 2, 64, 128, 1024], P(None, None, None, 'gy', 'gx'), may hold values from 0.15 to 0.85
- adjoint_end: float32 [2, 64, 128, 1024], P(None, None, 'gy', 'gx'), may hold values from -6 to 6
- rate_field: float32 [64, 128, 1024], P(None, 'gy', 'gx'), may hold values from 0.5 to 5
Outputs:
- adjoint_start: float32 [2, 64, 128, 1024], P(None, None, 'gy', 'gx')
- rate_grad: float32 [64, 128, 1024], P(None, 'gy', 'gx')
The draws below stay inside these ranges and needn't reach their ends.
All inputs are finite; a program needn't handle non-finite values.
Results may differ from the reference program's by a relative error of at most 0.00023.
Values sent between devices are 32-bit elements; how exact they have to be, the bound alone decides.
A program may use at most 128 MiB of HBM per device.

```python
import math
import jax
import jax.numpy as jnp

NZ = 64
FRAMES = 2
STEPS = 3
NX = 1024
NY = 128


def steps_of(rng, shape, shards, low, high):
    loudness, own = 1.0, jax.random.fold_in(rng, 6)
    for dim, blocks in shards:
        draws = jnp.exp(jax.random.uniform(jax.random.fold_in(own, dim), (blocks,), jnp.float32, low / len(shards), high / len(shards)))
        loudness = loudness * jnp.repeat(draws, shape[dim] // blocks).reshape([-1 if axis == dim else 1 for axis in range(len(shape))])
    return loudness


def centred(key, shape, deviation, most, pieces=(), held_as=jnp.bfloat16):
    entries = jax.random.normal(key, shape, jnp.float32) * deviation
    if len(pieces) > 0:
        entries = steps_of(key, shape, pieces, -0.22, 0.18) * entries
    return jnp.clip(entries, min=-most, max=most).astype(held_as)


def setup_inputs(seed: int = 0) -> dict:
    splits = jax.random.split(jax.random.key(seed), 4)
    return {
        "saved_conc": jnp.clip(0.15 + 0.70000002 * jax.random.uniform(splits[0], (STEPS, FRAMES, NZ, NY, NX), jnp.float32) ** steps_of(splits[0], (STEPS, FRAMES, NZ, NY, NX), ((3, 16), (4, 8)), -0.2, 0.2), 0.15, 0.85),
        "adjoint_end": centred(splits[1], (FRAMES, NZ, NY, NX), 1.0, 6.0, ((2, 16), (3, 8)), jnp.float32),
        "rate_field": jnp.clip(jnp.exp(math.log(5.0) - 2.3025851 * jax.random.uniform(splits[2], (NZ, NY, NX), jnp.float32) ** steps_of(splits[2], (NZ, NY, NX), ((1, 16), (2, 8)), -0.2, 0.2)), 0.5, 5.0),
    }


mix_energy = 2.5
grad_energy = 1.0
time_step = 0.1
diff_step = 0.03
bath_potential = 0.5


def laplace_z(field):
    diffs = field[..., 1:, :, :] - field[..., :-1, :, :]
    zeros = jnp.zeros_like(field[..., :1, :, :])
    return jnp.concatenate([diffs, zeros], axis=-3) - jnp.concatenate([zeros, diffs], axis=-3)


def laplace(field):
    total = jnp.roll(field, 1, -1) + jnp.roll(field, -1, -1) + jnp.roll(field, 1, -2) + jnp.roll(field, -1, -2)
    return total - 4.0 * field + laplace_z(field)


def potential(conc):
    return jnp.log(conc / (1.0 - conc)) + mix_energy * (1.0 - 2.0 * conc) - grad_energy * laplace(conc)


def flux_div(mobility, scaled):
    total = jnp.zeros_like(scaled)
    for axis in (-1, -2):
        flux = 0.5 * (mobility + jnp.roll(mobility, -1, axis)) * (jnp.roll(scaled, -1, axis) - scaled)
        total = total + flux - jnp.roll(flux, 1, axis)
    flux_z = 0.5 * (mobility[..., 1:, :, :] + mobility[..., :-1, :, :]) * (scaled[..., 1:, :, :] - scaled[..., :-1, :, :])
    zeros = jnp.zeros_like(scaled[..., :1, :, :])
    return total + jnp.concatenate([flux_z, zeros], axis=-3) - jnp.concatenate([zeros, flux_z], axis=-3)


def face_terms(chem, scaled):
    total = jnp.zeros_like(scaled)
    for axis in (-1, -2):
        term = -0.5 * (jnp.roll(chem, -1, axis) - chem) * (jnp.roll(scaled, -1, axis) - scaled)
        total = total + term + jnp.roll(term, 1, axis)
    term_z = -0.5 * (chem[..., 1:, :, :] - chem[..., :-1, :, :]) * (scaled[..., 1:, :, :] - scaled[..., :-1, :, :])
    zeros = jnp.zeros_like(scaled[..., :1, :, :])
    return total + jnp.concatenate([term_z, zeros], axis=-3) + jnp.concatenate([zeros, term_z], axis=-3)


def reference(saved_conc, adjoint_end, rate_field):
    adjoint = adjoint_end
    rate_grad = jnp.zeros(rate_field.shape, jnp.float32)
    for back in range(STEPS):
        conc = saved_conc[STEPS - 1 - back]
        chem = potential(conc)
        scaled = diff_step * adjoint
        g_pot = flux_div(conc * (1.0 - conc), scaled) - time_step * rate_field * adjoint
        faces = face_terms(chem, scaled)
        rate_grad = rate_grad + time_step * jnp.sum(adjoint * (bath_potential - chem), axis=0)
        curve = 1.0 / (conc * (1.0 - conc)) - 2.0 * mix_energy
        adjoint = adjoint + (1.0 - 2.0 * conc) * faces + curve * g_pot - grad_energy * laplace(g_pot)
    return adjoint, rate_grad
```

```python
import jax
import jax.numpy as jnp
from jax import lax
from jax.experimental import pallas as pl
from jax.experimental.pallas import tpu as pltpu
from jax.sharding import PartitionSpec as P

MESH = pl.DeviceIdType.MESH
DIRS = ((1, 0), (-1, 0), (0, 1), (0, -1), (1, 1), (1, -1), (-1, 1), (-1, -1))
ADJ, RATE, C, NEXT = 0, 2, (4, 3, 1), (0, 5, 6)
HALO, PAD = 2, 16


def body(sizes, conc_hbm, adj_hbm, rate_hbm, out_hbm, grad_hbm,
         raw, raw_rate, field, mob, pot, inv, gpot, part, acc, outs,
         load_sem, store_sem, send_sem, recv_sem):
    ngx, ngy, rows, cols, depth = sizes
    gx, gy = lax.axis_index("gx"), lax.axis_index("gy")
    lo, hi = HALO, HALO + rows
    xl, xh = PAD, PAD + cols

    def device(dy, dx):
        return (lax.rem(gx + dx + ngx, ngx), lax.rem(gy + dy + ngy, ngy))

    barrier = pltpu.get_barrier_semaphore()
    for dy, dx in DIRS:
        pl.semaphore_signal(barrier, inc=1, device_id=device(dy, dx), device_id_type=MESH)

    loads = []
    for slot, src in enumerate((adj_hbm, conc_hbm.at[2], rate_hbm, conc_hbm.at[1], conc_hbm.at[0])):
        group = []
        for y in range(rows):
            dst = raw_rate.at[y] if slot == RATE else raw.at[slot, y]
            group.append(pltpu.make_async_copy(src.at[:, y, :], dst, load_sem.at[slot, y]))
            group[-1].start()
        loads.append(group)

    def flip(slot):
        for y in range(rows):
            loads[slot][y].wait()
            if slot == RATE:
                half = (0.1 * raw_rate[y]).T
                tile = jnp.concatenate([half, half], axis=-1)
            else:
                tile = raw[slot, y].T
            field[slot, lo + y, xl:xh, :] = tile

    lane = lax.broadcasted_iota(jnp.int32, (8, 128), 1)
    upper = lax.rem(lane, depth) != depth - 1

    def mask(v):
        keep = jnp.broadcast_to(upper[:1], v.shape)
        return jnp.where(keep, v, 0.0)

    def up(v):
        return pltpu.roll(v, 127, 1)

    def down(v):
        return pltpu.roll(v, 1, 1)

    def laplace(ref, index, y, x, n):
        v = ref[(*index, y, pl.ds(x, n))]
        sides = (ref[(*index, y, pl.ds(x - 1, n))] + ref[(*index, y, pl.ds(x + 1, n))]
                 + ref[(*index, y - 1, pl.ds(x, n))] + ref[(*index, y + 1, pl.ds(x, n))])
        step = mask(up(v) - v)
        return v, sides - 4.0 * v + (step - down(step))

    def mobility(n, y, pieces):
        for x, w in pieces:
            c = field[C[n], y, pl.ds(x, w)]
            mob[n, y, pl.ds(x, w)] = c * (1.0 - c)

    def chem(n, y, pieces):
        for x, w in pieces:
            c, lap = laplace(field, (C[n],), y, x, w)
            m = c * (1.0 - c)
            r = 1.0 / m
            mob[n, y, pl.ds(x, w)] = m
            inv[n, y, pl.ds(x, w)] = r
            pot[n, y, pl.ds(x, w)] = jnp.log(c * c * r) + 2.5 * (1.0 - 2.0 * c) - lap

    def gflux(n, y, pieces):
        src = NEXT[2 - n]
        for x, w in pieces:
            b, m, u = field[src, y, pl.ds(x, w)], mob[n, y, pl.ds(x, w)], pot[n, y, pl.ds(x, w)]
            step = mask(up(b) - b)
            flux = (up(m) + m) * step
            term = (up(u) - u) * step
            g, q = flux - down(flux), term + down(term)
            for dy, dx in ((0, 1), (0, -1), (1, 0), (-1, 0)):
                at = (y + dy, pl.ds(x + dx, w))
                d = field[(src, *at)] - b
                g = g + (mob[(n, *at)] + m) * d
                q = q + (pot[(n, *at)] - u) * d
            g = 0.015 * g - field[RATE, y, pl.ds(x, w)] * b
            gpot[y, pl.ds(x, w)] = g
            c = field[C[n], y, pl.ds(x, w)]
            part[y, pl.ds(x, w)] = b - (0.015 * (1.0 - 2.0 * c)) * q + (inv[n, y, pl.ds(x, w)] - 5.0) * g

    def update(n, y, pieces):
        for x, w in pieces:
            _, lap = laplace(gpot, (), y, x, w)
            new = part[y, pl.ds(x, w)] - lap
            if n == 0:
                acc[1, y - lo, pl.ds(x - xl, w)] = new
            else:
                field[NEXT[3 - n], y, pl.ds(x, w)] = new

    def grad(n, y, _):
        for x in range(0, cols, 64):
            s = field[NEXT[2 - n], y, pl.ds(xl + x, 64)] * (0.5 - pot[n, y, pl.ds(xl + x, 64)])
            if n < 2:
                s = s + acc[0, y - lo, pl.ds(x, 64)]
            acc[0, y - lo, pl.ds(x, 64)] = s

    FULL = ((8, 48), (56, 48), (104, 48))
    OWN = ((16, 64), (80, 64))
    INNER = ((17, 64), (79, 64))
    CORE = ((18, 64), (78, 64))
    MAIN = ((24, 56), (80, 56))
    WIDE = ((8, 16), (136, 16))
    EDGE = ((16, 8), (136, 8))

    def rows_of(fn, n, first, count, pieces, gap=0):
        def one(k, _):
            fn(n, first + k + (gap * (k // (count // 2)) if gap else 0), pieces)
            return 0
        lax.fori_loop(0, count, one, 0)

    def message(which, k, fields, dy, dx, width, sem):
        ys = {1: (hi - width, lo - width), -1: (lo, hi), 0: (lo, lo)}[dy]
        xs = {1: (xh - HALO, xl - HALO), -1: (xl, xh), 0: (xl, xl)}[dx]
        h = rows if dy == 0 else width
        w = cols if dx == 0 else HALO
        f = pl.ds(*fields)
        return pltpu.make_async_remote_copy(
            src_ref=field.at[f, pl.ds(ys[0], h), pl.ds(xs[0], w)],
            dst_ref=field.at[f, pl.ds(ys[1], h), pl.ds(xs[1], w)],
            send_sem=send_sem.at[sem], recv_sem=recv_sem.at[sem],
            device_id=device(dy, dx), device_id_type=MESH)

    for slot in range(5):
        flip(slot)
    for n in (2, 1, 0):
        rows_of(mobility, n, lo, 1, OWN)
        rows_of(mobility, n, hi - 1, 1, OWN)
        rows_of(chem, n, lo + 1, rows - 2, INNER)

    pl.semaphore_wait(barrier, len(DIRS))
    first = []
    for k, (dy, dx) in enumerate(DIRS):
        if dx == 0:
            first.append(message(0, k, (0, 2), dy, dx, 2, k))
            first.append(message(0, k, (2, 1), dy, dx, 1, 8 + k))
        else:
            first.append(message(0, k, (0, 3), dy, dx, 2, k))
    later = [message(1, k, (3, 2), dy, dx, 2, 16 + k) for k, (dy, dx) in enumerate(DIRS)]
    for copy in first + later:
        copy.start()

    def before(n):
        rows_of(gflux, n, lo + 1, rows - 2, CORE)
        rows_of(update, n, lo + 2, rows - 4, MAIN)

    def rim(n):
        rows_of(mobility, n, lo - 2, 1, FULL)
        rows_of(mobility, n, hi + 1, 1, FULL)
        rows_of(chem, n, lo - 1, 4, FULL, 6)
        rows_of(chem, n, lo + 1, rows - 2, WIDE)

    def after(n):
        if n == 2:
            rows_of(gflux, n, lo - 1, 6, FULL, 4)
        else:
            rows_of(gflux, n, lo - 1, 4, FULL, 6)
        rows_of(gflux, n, lo + 1, rows - 2, WIDE)
        rows_of(update, n, lo, 4, OWN, 4)
        rows_of(update, n, lo + 2, rows - 4, EDGE)

    before(2)
    for copy in first:
        copy.wait_recv()
    rim(2)
    after(2)
    second = [message(2, k, (5, 1), dy, dx, 2, 24 + k) for k, (dy, dx) in enumerate(DIRS)]
    for copy in second:
        copy.start()
    rows_of(grad, 2, lo, rows, ())
    for copy in later:
        copy.wait_recv()
    rim(1)
    before(1)
    rim(0)
    rows_of(grad, 1, lo, rows, ())
    for copy in second:
        copy.wait_recv()
    after(1)
    third = [message(3, k, (6, 1), dy, dx, 2, 32 + k) for k, (dy, dx) in enumerate(DIRS)]
    for copy in third:
        copy.start()
    before(0)
    rows_of(grad, 0, lo, rows, ())
    stores = []
    for y in range(rows):
        s = acc[0, y]
        s = 0.1 * (s + pltpu.roll(s, depth, 1))
        outs[0, y] = s.T
        stores.append(pltpu.make_async_copy(outs.at[0, y, pl.ds(0, depth)], grad_hbm.at[:, y, :], store_sem.at[0, y]))
        stores[-1].start()
    for copy in third:
        copy.wait_recv()
    after(0)
    for y in range(rows):
        outs[1, y] = acc[1, y].T
        stores.append(pltpu.make_async_copy(outs.at[1, y], out_hbm.at[:, y, :], store_sem.at[1, y]))
        stores[-1].start()
    for copy in first + later + second + third:
        copy.wait_send()
    for copy in stores:
        copy.wait()


def solution(mesh):
    ngx, ngy = mesh.shape["gx"], mesh.shape["gy"]

    def shards(saved_conc, adjoint_end, rate_field):
        steps, frames, depth, rows, cols = saved_conc.shape
        lanes = frames * depth
        conc = saved_conc.reshape(steps, lanes, rows, cols)
        adj = adjoint_end.reshape(lanes, rows, cols)
        ext = (rows + 2 * HALO, cols + 2 * PAD, lanes)

        def kernel(*refs):
            body((ngx, ngy, rows, cols, depth), *refs)

        hbm = pl.BlockSpec(memory_space=pl.ANY)
        out, grad = pl.pallas_call(
            kernel,
            out_shape=(jax.ShapeDtypeStruct((lanes, rows, cols), jnp.float32),
                       jax.ShapeDtypeStruct((depth, rows, cols), jnp.float32)),
            in_specs=[hbm] * 3, out_specs=(hbm, hbm),
            scratch_shapes=[
                pltpu.VMEM((5, rows, lanes, cols), jnp.float32),
                pltpu.VMEM((rows, depth, cols), jnp.float32),
                pltpu.VMEM((7, *ext), jnp.float32),
                pltpu.VMEM((3, *ext), jnp.float32),
                pltpu.VMEM((3, *ext), jnp.float32),
                pltpu.VMEM((3, *ext), jnp.float32),
                pltpu.VMEM(ext, jnp.float32),
                pltpu.VMEM(ext, jnp.float32),
                pltpu.VMEM((2, rows, cols, lanes), jnp.float32),
                pltpu.VMEM((2, rows, lanes, cols), jnp.float32),
                pltpu.SemaphoreType.DMA((5, rows)),
                pltpu.SemaphoreType.DMA((2, rows)),
                pltpu.SemaphoreType.DMA((40,)),
                pltpu.SemaphoreType.DMA((40,)),
            ],
            compiler_params=pltpu.CompilerParams(
                collective_id=0, has_side_effects=True, vmem_limit_bytes=56 << 20),
        )(conc, adj, rate_field)
        return out.reshape(adjoint_end.shape), grad

    return jax.shard_map(
        shards, mesh=mesh,
        in_specs=(P(None, None, None, "gy", "gx"), P(None, None, "gy", "gx"), P(None, "gy", "gx")),
        out_specs=(P(None, None, "gy", "gx"), P(None, "gy", "gx")),
        check_vma=False)
```

```python
import jax
import jax.numpy as jnp
from jax import lax
from jax.experimental import pallas as pl
from jax.experimental.pallas import tpu as pltpu
from jax.sharding import PartitionSpec as P

MESH = pl.DeviceIdType.MESH
DIRS = ((1, 1), (1, -1), (-1, 1), (-1, -1), (0, 1), (0, -1), (1, 0), (-1, 0))
ADJ, RATE, C, NEXT = 0, 2, (4, 3, 1), (0, 5, 6)
UNROLL = (4, 3, 2, 1)
HALO, PAD = 2, 16


def body(sizes, conc_hbm, adj_hbm, rate_hbm, out_hbm, grad_hbm,
         raw, raw_rate, field, mob, pot, inv, gpot, part, acc, outs,
         load_sem, store_sem, send_sem, recv_sem):
    ngx, ngy, rows, cols, depth = sizes
    gx, gy = lax.axis_index("gx"), lax.axis_index("gy")
    lo, hi = HALO, HALO + rows
    xl, xh = PAD, PAD + cols

    def device(dy, dx):
        return (lax.rem(gx + dx + ngx, ngx), lax.rem(gy + dy + ngy, ngy))

    barrier = pltpu.get_barrier_semaphore()
    for dy, dx in DIRS:
        pl.semaphore_signal(barrier, inc=1, device_id=device(dy, dx), device_id_type=MESH)

    loads = []
    for slot, src in enumerate((adj_hbm, conc_hbm.at[2], rate_hbm, conc_hbm.at[1], conc_hbm.at[0])):
        group = []
        for y in range(rows):
            dst = raw_rate.at[y] if slot == RATE else raw.at[slot, y]
            group.append(pltpu.make_async_copy(src.at[:, y, :], dst, load_sem.at[slot, y]))
            group[-1].start()
        loads.append(group)

    def flip(slot):
        for y in range(rows):
            loads[slot][y].wait()
            if slot == RATE:
                half = (0.1 * raw_rate[y]).T
                tile = jnp.concatenate([half, half], axis=-1)
            else:
                tile = raw[slot, y].T
            field[slot, lo + y, xl:xh, :] = tile

    lane = lax.broadcasted_iota(jnp.int32, (8, 128), 1)
    upper, lower = lax.rem(lane, depth) != depth - 1, lax.rem(lane, depth) != 0

    def pick(keep, v, other):
        return jnp.where(jnp.broadcast_to(keep[:1], v.shape), v, other)

    def up(v):
        return pltpu.roll(v, 127, 1)

    def down(v):
        return pltpu.roll(v, 1, 1)

    def laplace(ref, index, y, x, n):
        v = ref[(*index, y, pl.ds(x, n))]
        sides = (ref[(*index, y, pl.ds(x - 1, n))] + ref[(*index, y, pl.ds(x + 1, n))]
                 + ref[(*index, y - 1, pl.ds(x, n))] + ref[(*index, y + 1, pl.ds(x, n))])
        return v, sides - 6.0 * v + (pick(upper, up(v), v) + pick(lower, down(v), v))

    def mobility(n, y, pieces):
        for x, w in pieces:
            c = field[C[n], y, pl.ds(x, w)]
            mob[n, y, pl.ds(x, w)] = c * (1.0 - c)

    def chem(n, y, pieces):
        for x, w in pieces:
            c, lap = laplace(field, (C[n],), y, x, w)
            m = c * (1.0 - c)
            r = 1.0 / m
            mob[n, y, pl.ds(x, w)] = m
            inv[n, y, pl.ds(x, w)] = r
            pot[n, y, pl.ds(x, w)] = jnp.log(c * c * r) + 2.5 * (1.0 - 2.0 * c) - lap

    def gflux(n, y, pieces):
        src = NEXT[2 - n]
        for x, w in pieces:
            b, m, u = field[src, y, pl.ds(x, w)], mob[n, y, pl.ds(x, w)], pot[n, y, pl.ds(x, w)]
            step = pick(upper, up(b) - b, 0.0)
            flux = (up(m) + m) * step
            term = (up(u) - u) * step
            g, q = flux - down(flux), term + down(term)
            for dy, dx in ((0, 1), (0, -1), (1, 0), (-1, 0)):
                at = (y + dy, pl.ds(x + dx, w))
                d = field[(src, *at)] - b
                g = g + (mob[(n, *at)] + m) * d
                q = q + (pot[(n, *at)] - u) * d
            g = 0.015 * g - field[RATE, y, pl.ds(x, w)] * b
            gpot[y, pl.ds(x, w)] = g
            c = field[C[n], y, pl.ds(x, w)]
            part[y, pl.ds(x, w)] = b - (0.015 * (1.0 - 2.0 * c)) * q + (inv[n, y, pl.ds(x, w)] - 5.0) * g

    def update(n, y, pieces):
        for x, w in pieces:
            _, lap = laplace(gpot, (), y, x, w)
            new = part[y, pl.ds(x, w)] - lap
            if n == 0:
                acc[1, y - lo, pl.ds(x - xl, w)] = new
            else:
                field[NEXT[3 - n], y, pl.ds(x, w)] = new

    def grad(n, y, _):
        for x in range(0, cols, 64):
            s = field[NEXT[2 - n], y, pl.ds(xl + x, 64)] * (0.5 - pot[n, y, pl.ds(xl + x, 64)])
            if n < 2:
                s = s + acc[0, y - lo, pl.ds(x, 64)]
            acc[0, y - lo, pl.ds(x, 64)] = s

    FULL = ((8, 144),)
    OWN = ((16, 128),)
    INNER = ((17, 64), (79, 64))
    CORE = ((18, 64), (78, 64))
    MAIN = ((24, 112),)
    WIDE = ((8, 16), (136, 16))
    EDGE = ((16, 8), (136, 8))

    def rows_of(fn, n, first, count, pieces, gap=0):
        step = next(u for u in UNROLL if count % u == 0)

        def some(k, _):
            for i in range(step):
                r = k * step + i
                fn(n, first + r + (gap * (r // (count // 2)) if gap else 0), pieces)
            return 0

        if step == count:
            some(0, 0)
        else:
            lax.fori_loop(0, count // step, some, 0)

    def message(fields, dy, dx, sem, ring=HALO):
        ring = 1 if dy and dx else ring
        ys = {1: (hi - ring, lo - ring), -1: (lo, hi), 0: (lo, lo)}[dy]
        xs = {1: (xh - ring, xl - ring), -1: (xl, xh), 0: (xl, xl)}[dx]
        h = ring if dy else rows
        w = ring if dx else cols
        f = pl.ds(*fields)
        return pltpu.make_async_remote_copy(
            src_ref=field.at[f, pl.ds(ys[0], h), pl.ds(xs[0], w)],
            dst_ref=field.at[f, pl.ds(ys[1], h), pl.ds(xs[1], w)],
            send_sem=send_sem.at[sem], recv_sem=recv_sem.at[sem],
            device_id=device(dy, dx), device_id_type=MESH)

    for slot in range(3):
        flip(slot)
    pl.semaphore_wait(barrier, len(DIRS))
    first = []
    for k, (dy, dx) in enumerate(DIRS):
        if dx == 0:
            first.append(message((0, 2), dy, dx, k))
            first.append(message((2, 1), dy, dx, 32 + k, 1))
        else:
            first.append(message((0, 3), dy, dx, k))
    for copy in first:
        copy.start()
    for slot in range(3, 5):
        flip(slot)
    later = [message((3, 2), dy, dx, 8 + k) for k, (dy, dx) in enumerate(DIRS)]
    for copy in later:
        copy.start()

    def local(n):
        rows_of(mobility, n, lo, 2, OWN, rows - 2)
        rows_of(chem, n, lo + 1, rows - 2, INNER)

    def before(n):
        rows_of(gflux, n, lo + 1, rows - 2, CORE)
        rows_of(update, n, lo + 2, rows - 4, MAIN)

    def rim(n):
        rows_of(mobility, n, lo - 2, 2, FULL, rows + 2)
        rows_of(chem, n, lo - 1, 4, FULL, 6)
        rows_of(chem, n, lo + 1, rows - 2, WIDE)

    def after(n):
        if n == 2:
            rows_of(gflux, n, lo - 1, 6, FULL, 4)
        else:
            rows_of(gflux, n, lo - 1, 4, FULL, 6)
        rows_of(gflux, n, lo + 1, rows - 2, WIDE)
        rows_of(update, n, lo, 4, OWN, 4)
        rows_of(update, n, lo + 2, rows - 4, EDGE)

    local(2)
    before(2)
    local(1)
    local(0)
    for copy in first:
        copy.wait_recv()
    rim(2)
    after(2)
    second = [message((5, 1), dy, dx, 16 + k) for k, (dy, dx) in enumerate(DIRS)]
    for copy in second:
        copy.start()
    rows_of(grad, 2, lo, rows, ())
    for copy in later:
        copy.wait_recv()
    rim(1)
    before(1)
    rim(0)
    rows_of(grad, 1, lo, rows, ())
    for copy in second:
        copy.wait_recv()
    after(1)
    third = [message((6, 1), dy, dx, 24 + k) for k, (dy, dx) in enumerate(DIRS)]
    for copy in third:
        copy.start()
    before(0)
    rows_of(grad, 0, lo, rows, ())
    stores = []
    for y in range(rows):
        s = acc[0, y]
        s = 0.1 * (s + pltpu.roll(s, depth, 1))
        outs[0, y] = s.T
        stores.append(pltpu.make_async_copy(outs.at[0, y, pl.ds(0, depth)], grad_hbm.at[:, y, :], store_sem.at[0, y]))
        stores[-1].start()
    for copy in third:
        copy.wait_recv()
    after(0)
    for y in range(rows):
        outs[1, y] = acc[1, y].T
        stores.append(pltpu.make_async_copy(outs.at[1, y], out_hbm.at[:, y, :], store_sem.at[1, y]))
        stores[-1].start()
    for copy in first + later + second + third:
        copy.wait_send()
    for copy in stores:
        copy.wait()


def solution(mesh):
    ngx, ngy = mesh.shape["gx"], mesh.shape["gy"]

    def shards(saved_conc, adjoint_end, rate_field):
        steps, frames, depth, rows, cols = saved_conc.shape
        lanes = frames * depth
        conc = saved_conc.reshape(steps, lanes, rows, cols)
        adj = adjoint_end.reshape(lanes, rows, cols)
        ext = (rows + 2 * HALO, cols + 2 * PAD, lanes)

        def kernel(*refs):
            body((ngx, ngy, rows, cols, depth), *refs)

        hbm = pl.BlockSpec(memory_space=pl.ANY)
        out, grad = pl.pallas_call(
            kernel,
            out_shape=(jax.ShapeDtypeStruct((lanes, rows, cols), jnp.float32),
                       jax.ShapeDtypeStruct((depth, rows, cols), jnp.float32)),
            in_specs=[hbm] * 3, out_specs=(hbm, hbm),
            scratch_shapes=[
                pltpu.VMEM((5, rows, lanes, cols), jnp.float32),
                pltpu.VMEM((rows, depth, cols), jnp.float32),
                pltpu.VMEM((7, *ext), jnp.float32),
                pltpu.VMEM((3, *ext), jnp.float32),
                pltpu.VMEM((3, *ext), jnp.float32),
                pltpu.VMEM((3, *ext), jnp.float32),
                pltpu.VMEM(ext, jnp.float32),
                pltpu.VMEM(ext, jnp.float32),
                pltpu.VMEM((2, rows, cols, lanes), jnp.float32),
                pltpu.VMEM((2, rows, lanes, cols), jnp.float32),
                pltpu.SemaphoreType.DMA((5, rows)),
                pltpu.SemaphoreType.DMA((2, rows)),
                pltpu.SemaphoreType.DMA((40,)),
                pltpu.SemaphoreType.DMA((40,)),
            ],
            compiler_params=pltpu.CompilerParams(
                collective_id=0, has_side_effects=True, vmem_limit_bytes=56 << 20),
        )(conc, adj, rate_field)
        return out.reshape(adjoint_end.shape), grad

    return jax.shard_map(
        shards, mesh=mesh,
        in_specs=(P(None, None, None, "gy", "gx"), P(None, None, "gy", "gx"), P(None, "gy", "gx")),
        out_specs=(P(None, None, "gy", "gx"), P(None, "gy", "gx")),
        check_vma=False)
```

```python
import functools

import jax
import jax.numpy as jnp
from jax import lax
from jax.experimental import pallas as pl
from jax.experimental.pallas import tpu as pltpu
from jax.sharding import PartitionSpec as P

MESH = pl.DeviceIdType.MESH
DIRS = ((1, 1), (1, -1), (-1, 1), (-1, -1), (0, 1), (0, -1), (1, 0), (-1, 0))
ADJ, RATE, C, NEXT = 0, 2, (4, 3, 1), (0, 5, 6)
UNROLL = (4, 3, 2, 1)
HALO, PAD = 2, 16


def body(sizes, conc_hbm, adj_hbm, rate_hbm, last, acc,
         raw, raw_rate, field, mob, pot, inv, gpot, part,
         load_sem, send_sem, recv_sem):
    ngx, ngy, rows, cols, depth = sizes
    gx, gy = lax.axis_index("gx"), lax.axis_index("gy")
    lo, hi = HALO, HALO + rows
    xl, xh = PAD, PAD + cols

    def device(dy, dx):
        return (lax.rem(gx + dx + ngx, ngx), lax.rem(gy + dy + ngy, ngy))

    barrier = pltpu.get_barrier_semaphore()
    for dy, dx in DIRS:
        pl.semaphore_signal(barrier, inc=1, device_id=device(dy, dx), device_id_type=MESH)

    loads = []
    for slot, src in enumerate((adj_hbm, conc_hbm.at[2], rate_hbm, conc_hbm.at[1], conc_hbm.at[0])):
        group = []
        for y in range(rows):
            dst = raw_rate.at[y] if slot == RATE else raw.at[slot, y]
            group.append(pltpu.make_async_copy(src.at[:, y, :], dst, load_sem.at[slot, y]))
            group[-1].start()
        loads.append(group)

    def flip(slot):
        for y in range(rows):
            loads[slot][y].wait()
            if slot == RATE:
                half = (0.1 * raw_rate[y]).T
                tile = jnp.concatenate([half, half], axis=-1)
            else:
                tile = raw[slot, y].T
            field[slot, lo + y, xl:xh, :] = tile

    lane = lax.broadcasted_iota(jnp.int32, (8, 128), 1)
    upper, lower = lax.rem(lane, depth) != depth - 1, lax.rem(lane, depth) != 0

    def pick(keep, v, other):
        return jnp.where(jnp.broadcast_to(keep[:1], v.shape), v, other)

    def up(v):
        return pltpu.roll(v, 127, 1)

    def down(v):
        return pltpu.roll(v, 1, 1)

    def laplace(ref, index, y, x, n):
        v = ref[(*index, y, pl.ds(x, n))]
        sides = (ref[(*index, y, pl.ds(x - 1, n))] + ref[(*index, y, pl.ds(x + 1, n))]
                 + ref[(*index, y - 1, pl.ds(x, n))] + ref[(*index, y + 1, pl.ds(x, n))])
        return v, sides - 6.0 * v + (pick(upper, up(v), v) + pick(lower, down(v), v))

    def mobility(n, y, pieces):
        for x, w in pieces:
            c = field[C[n], y, pl.ds(x, w)]
            mob[n, y, pl.ds(x, w)] = c * (1.0 - c)

    def chem(n, y, pieces):
        for x, w in pieces:
            c, lap = laplace(field, (C[n],), y, x, w)
            m = c * (1.0 - c)
            r = 1.0 / m
            mob[n, y, pl.ds(x, w)] = m
            inv[n, y, pl.ds(x, w)] = r
            pot[n, y, pl.ds(x, w)] = jnp.log(c * c * r) + 2.5 * (1.0 - 2.0 * c) - lap

    def gflux(n, y, pieces):
        src = NEXT[2 - n]
        for x, w in pieces:
            b, m, u = field[src, y, pl.ds(x, w)], mob[n, y, pl.ds(x, w)], pot[n, y, pl.ds(x, w)]
            step = pick(upper, up(b) - b, 0.0)
            flux = (up(m) + m) * step
            term = (up(u) - u) * step
            g, q = flux - down(flux), term + down(term)
            for dy, dx in ((0, 1), (0, -1), (1, 0), (-1, 0)):
                at = (y + dy, pl.ds(x + dx, w))
                d = field[(src, *at)] - b
                g = g + (mob[(n, *at)] + m) * d
                q = q + (pot[(n, *at)] - u) * d
            g = 0.015 * g - field[RATE, y, pl.ds(x, w)] * b
            gpot[y, pl.ds(x, w)] = g
            c = field[C[n], y, pl.ds(x, w)]
            part[y, pl.ds(x, w)] = b - (0.015 * (1.0 - 2.0 * c)) * q + (inv[n, y, pl.ds(x, w)] - 5.0) * g

    def update(n, y, pieces):
        for x, w in pieces:
            _, lap = laplace(gpot, (), y, x, w)
            new = part[y, pl.ds(x, w)] - lap
            if n == 0:
                last[y - lo, pl.ds(x - xl, w)] = new
            else:
                field[NEXT[3 - n], y, pl.ds(x, w)] = new

    def grad(n, y, _):
        for x in range(0, cols, 64):
            s = field[NEXT[2 - n], y, pl.ds(xl + x, 64)] * (0.5 - pot[n, y, pl.ds(xl + x, 64)])
            if n < 2:
                s = s + acc[y - lo, pl.ds(x, 64)]
            acc[y - lo, pl.ds(x, 64)] = s

    FULL = ((8, 144),)
    OWN = ((16, 128),)
    INNER = ((17, 64), (79, 64))
    CORE = ((18, 64), (78, 64))
    MAIN = ((24, 112),)
    WIDE = ((8, 16), (136, 16))
    EDGE = ((16, 8), (136, 8))

    def rows_of(fn, n, first, count, pieces, gap=0):
        step = next(u for u in UNROLL if count % u == 0)

        def some(k, _):
            for i in range(step):
                r = k * step + i
                fn(n, first + r + (gap * (r // (count // 2)) if gap else 0), pieces)
            return 0

        if step == count:
            some(0, 0)
        else:
            lax.fori_loop(0, count // step, some, 0)

    def message(fields, dy, dx, sem, ring=HALO):
        ring = 1 if dy and dx else ring
        ys = {1: (hi - ring, lo - ring), -1: (lo, hi), 0: (lo, lo)}[dy]
        xs = {1: (xh - ring, xl - ring), -1: (xl, xh), 0: (xl, xl)}[dx]
        h = ring if dy else rows
        w = ring if dx else cols
        f = pl.ds(*fields)
        return pltpu.make_async_remote_copy(
            src_ref=field.at[f, pl.ds(ys[0], h), pl.ds(xs[0], w)],
            dst_ref=field.at[f, pl.ds(ys[1], h), pl.ds(xs[1], w)],
            send_sem=send_sem.at[sem], recv_sem=recv_sem.at[sem],
            device_id=device(dy, dx), device_id_type=MESH)

    for slot in range(3):
        flip(slot)
    pl.semaphore_wait(barrier, len(DIRS))
    first = []
    for k, (dy, dx) in enumerate(DIRS):
        if dx == 0:
            first.append(message((0, 2), dy, dx, k))
            first.append(message((2, 1), dy, dx, 32 + k, 1))
        else:
            first.append(message((0, 3), dy, dx, k))
    for copy in first:
        copy.start()
    for slot in range(3, 5):
        flip(slot)
    later = [message((3, 2), dy, dx, 8 + k) for k, (dy, dx) in enumerate(DIRS)]
    for copy in later:
        copy.start()

    def local(n):
        rows_of(mobility, n, lo, 2, OWN, rows - 2)
        rows_of(chem, n, lo + 1, rows - 2, INNER)

    def before(n):
        rows_of(gflux, n, lo + 1, rows - 2, CORE)
        rows_of(update, n, lo + 2, rows - 4, MAIN)

    def rim(n):
        rows_of(mobility, n, lo - 2, 2, FULL, rows + 2)
        rows_of(chem, n, lo - 1, 4, FULL, 6)
        rows_of(chem, n, lo + 1, rows - 2, WIDE)

    def after(n):
        if n == 2:
            rows_of(gflux, n, lo - 1, 6, FULL, 4)
        else:
            rows_of(gflux, n, lo - 1, 4, FULL, 6)
        rows_of(gflux, n, lo + 1, rows - 2, WIDE)
        rows_of(update, n, lo, 4, OWN, 4)
        rows_of(update, n, lo + 2, rows - 4, EDGE)

    local(2)
    before(2)
    local(1)
    local(0)
    for copy in first:
        copy.wait_recv()
    rim(2)
    after(2)
    second = [message((5, 1), dy, dx, 16 + k) for k, (dy, dx) in enumerate(DIRS)]
    for copy in second:
        copy.start()
    rows_of(grad, 2, lo, rows, ())
    for copy in later:
        copy.wait_recv()
    rim(1)
    before(1)
    rim(0)
    rows_of(grad, 1, lo, rows, ())
    for copy in second:
        copy.wait_recv()
    after(1)
    third = [message((6, 1), dy, dx, 24 + k) for k, (dy, dx) in enumerate(DIRS)]
    for copy in third:
        copy.start()
    before(0)
    rows_of(grad, 0, lo, rows, ())
    for copy in third:
        copy.wait_recv()
    after(0)
    for copy in first + later + second + third:
        copy.wait_send()


def turn(rows, depth, new_ref, sum_ref, out_hbm, grad_hbm, outs, store_sem):
    stores = []
    for y in range(rows):
        outs[1, y] = new_ref[y].T
        s = sum_ref[y]
        outs[0, y] = (0.1 * (s + pltpu.roll(s, depth, 1))).T
        stores.append(pltpu.make_async_copy(outs.at[1, y], out_hbm.at[:, y, :], store_sem.at[1, y]))
        stores.append(pltpu.make_async_copy(outs.at[0, y, pl.ds(0, depth)], grad_hbm.at[:, y, :], store_sem.at[0, y]))
        for copy in stores[-2:]:
            copy.start()
    for copy in stores:
        copy.wait()


def solution(mesh):
    ngx, ngy = mesh.shape["gx"], mesh.shape["gy"]

    def shards(saved_conc, adjoint_end, rate_field):
        steps, frames, depth, rows, cols = saved_conc.shape
        lanes = frames * depth
        conc = saved_conc.reshape(steps, lanes, rows, cols)
        adj = adjoint_end.reshape(lanes, rows, cols)
        ext = (rows + 2 * HALO, cols + 2 * PAD, lanes)

        def kernel(*refs):
            body((ngx, ngy, rows, cols, depth), *refs)

        hbm = pl.BlockSpec(memory_space=pltpu.HBM)
        vmem = pl.BlockSpec(memory_space=pltpu.VMEM)
        tile = jax.ShapeDtypeStruct((rows, cols, lanes), jnp.float32)
        last, acc = pl.pallas_call(
            kernel,
            out_shape=(tile, tile),
            in_specs=[hbm] * 3, out_specs=(vmem, vmem),
            scratch_shapes=[
                pltpu.VMEM((5, rows, lanes, cols), jnp.float32),
                pltpu.VMEM((rows, depth, cols), jnp.float32),
                pltpu.VMEM((7, *ext), jnp.float32),
                pltpu.VMEM((3, *ext), jnp.float32),
                pltpu.VMEM((3, *ext), jnp.float32),
                pltpu.VMEM((3, *ext), jnp.float32),
                pltpu.VMEM(ext, jnp.float32),
                pltpu.VMEM(ext, jnp.float32),
                pltpu.SemaphoreType.DMA((5, rows)),
                pltpu.SemaphoreType.DMA((40,)),
                pltpu.SemaphoreType.DMA((40,)),
            ],
            compiler_params=pltpu.CompilerParams(
                collective_id=0, has_side_effects=True, vmem_limit_bytes=48 << 20),
        )(*(pltpu.with_memory_space_constraint(v, pltpu.HBM) for v in (conc, adj, rate_field)))
        out, grad = pl.pallas_call(
            functools.partial(turn, rows, depth),
            out_shape=(jax.ShapeDtypeStruct((lanes, rows, cols), jnp.float32),
                       jax.ShapeDtypeStruct((depth, rows, cols), jnp.float32)),
            in_specs=[vmem, vmem], out_specs=(hbm, hbm),
            scratch_shapes=[pltpu.VMEM((2, rows, lanes, cols), jnp.float32), pltpu.SemaphoreType.DMA((2, rows))],
            compiler_params=pltpu.CompilerParams(vmem_limit_bytes=8 << 20),
        )(last, acc)
        return out.reshape(adjoint_end.shape), grad

    return jax.shard_map(
        shards, mesh=mesh,
        in_specs=(P(None, None, None, "gy", "gx"), P(None, None, "gy", "gx"), P(None, "gy", "gx")),
        out_specs=(P(None, None, "gy", "gx"), P(None, "gy", "gx")),
        check_vma=False)
```

```python
import functools

import jax
import jax.numpy as jnp
from jax import lax
from jax.experimental import pallas as pl
from jax.experimental.pallas import tpu as pltpu
from jax.sharding import PartitionSpec as P

MESH = pl.DeviceIdType.MESH
DIRS = ((1, 1), (1, -1), (-1, 1), (-1, -1), (0, 1), (0, -1), (1, 0), (-1, 0))
ADJ, RATE, C, NEXT = 0, 2, (4, 3, 1), (0, 5, 6)
UNROLL = (4, 3, 2, 1)
HALO, PAD = 2, 16


def body(sizes, conc_hbm, adj_hbm, rate_hbm, last, acc,
         raw, raw_rate, field, mob, pot, inv, gpot, part,
         load_sem, send_sem, recv_sem):
    ngx, ngy, rows, cols, depth = sizes
    gx, gy = lax.axis_index("gx"), lax.axis_index("gy")
    lo, hi = HALO, HALO + rows
    xl, xh = PAD, PAD + cols

    def device(dy, dx):
        return (lax.rem(gx + dx + ngx, ngx), lax.rem(gy + dy + ngy, ngy))

    barrier = pltpu.get_barrier_semaphore()
    for dy, dx in DIRS:
        pl.semaphore_signal(barrier, inc=1, device_id=device(dy, dx), device_id_type=MESH)

    loads = []
    for slot, src in enumerate((adj_hbm, conc_hbm.at[2], rate_hbm, conc_hbm.at[1], conc_hbm.at[0])):
        group = []
        for y in range(rows):
            dst = raw_rate.at[y] if slot == RATE else raw.at[slot, y]
            group.append(pltpu.make_async_copy(src.at[:, y, :], dst, load_sem.at[slot, y]))
            group[-1].start()
        loads.append(group)

    def flip(slot):
        for y in range(rows):
            loads[slot][y].wait()
            if slot == RATE:
                half = (0.1 * raw_rate[y]).T
                tile = jnp.concatenate([half, half], axis=-1)
            else:
                tile = raw[slot, y].T
            field[slot, lo + y, xl:xh, :] = tile

    lane = lax.broadcasted_iota(jnp.int32, (8, 128), 1)
    upper, lower = lax.rem(lane, depth) != depth - 1, lax.rem(lane, depth) != 0

    def pick(keep, v, other):
        return jnp.where(jnp.broadcast_to(keep[:1], v.shape), v, other)

    def up(v):
        return pltpu.roll(v, 127, 1)

    def down(v):
        return pltpu.roll(v, 1, 1)

    def laplace(ref, index, y, x, n):
        v = ref[(*index, y, pl.ds(x, n))]
        sides = (ref[(*index, y, pl.ds(x - 1, n))] + ref[(*index, y, pl.ds(x + 1, n))]
                 + ref[(*index, y - 1, pl.ds(x, n))] + ref[(*index, y + 1, pl.ds(x, n))])
        return v, sides - 6.0 * v + (pick(upper, up(v), v) + pick(lower, down(v), v))

    def mobility(n, y, pieces):
        for x, w in pieces:
            c = field[C[n], y, pl.ds(x, w)]
            mob[n, y, pl.ds(x, w)] = c * (1.0 - c)

    def chem(n, y, pieces):
        for x, w in pieces:
            c, lap = laplace(field, (C[n],), y, x, w)
            m = c * (1.0 - c)
            r = 1.0 / m
            mob[n, y, pl.ds(x, w)] = m
            inv[n, y, pl.ds(x, w)] = r
            pot[n, y, pl.ds(x, w)] = jnp.log(c * c * r) + 2.5 * (1.0 - 2.0 * c) - lap

    def gflux(n, y, pieces):
        src = NEXT[2 - n]
        for x, w in pieces:
            b, m, u = field[src, y, pl.ds(x, w)], mob[n, y, pl.ds(x, w)], pot[n, y, pl.ds(x, w)]
            step = pick(upper, up(b) - b, 0.0)
            flux = (up(m) + m) * step
            term = (up(u) - u) * step
            g, q = flux - down(flux), term + down(term)
            for dy, dx in ((0, 1), (0, -1), (1, 0), (-1, 0)):
                at = (y + dy, pl.ds(x + dx, w))
                d = field[(src, *at)] - b
                g = g + (mob[(n, *at)] + m) * d
                q = q + (pot[(n, *at)] - u) * d
            g = 0.015 * g - field[RATE, y, pl.ds(x, w)] * b
            gpot[y, pl.ds(x, w)] = g
            c = field[C[n], y, pl.ds(x, w)]
            part[y, pl.ds(x, w)] = b - (0.015 * (1.0 - 2.0 * c)) * q + (inv[n, y, pl.ds(x, w)] - 5.0) * g

    def update(n, y, pieces):
        for x, w in pieces:
            _, lap = laplace(gpot, (), y, x, w)
            new = part[y, pl.ds(x, w)] - lap
            if n == 0:
                last[y - lo, pl.ds(x - xl, w)] = new
            else:
                field[NEXT[3 - n], y, pl.ds(x, w)] = new

    def grad(n, y, _):
        for x in range(0, cols, 64):
            s = field[NEXT[2 - n], y, pl.ds(xl + x, 64)] * (0.5 - pot[n, y, pl.ds(xl + x, 64)])
            if n < 2:
                s = s + acc[y - lo, pl.ds(x, 64)]
            acc[y - lo, pl.ds(x, 64)] = s

    FULL = ((8, 144),)
    OWN = ((16, 128),)
    INNER = ((17, 64), (79, 64))
    CORE = ((18, 64), (78, 64))
    MAIN = ((24, 112),)
    WIDE = ((8, 16), (136, 16))
    EDGE = ((16, 8), (136, 8))

    def rows_of(fn, n, first, count, pieces, gap=0):
        step = next(u for u in UNROLL if count % u == 0)

        def some(k, _):
            for i in range(step):
                r = k * step + i
                fn(n, first + r + (gap * (r // (count // 2)) if gap else 0), pieces)
            return 0

        if step == count:
            some(0, 0)
        else:
            lax.fori_loop(0, count // step, some, 0)

    def message(fields, dy, dx, sem, ring=HALO):
        ring = 1 if dy and dx else ring
        ys = {1: (hi - ring, lo - ring), -1: (lo, hi), 0: (lo, lo)}[dy]
        xs = {1: (xh - ring, xl - ring), -1: (xl, xh), 0: (xl, xl)}[dx]
        h = ring if dy else rows
        w = ring if dx else cols
        f = pl.ds(*fields)
        return pltpu.make_async_remote_copy(
            src_ref=field.at[f, pl.ds(ys[0], h), pl.ds(xs[0], w)],
            dst_ref=field.at[f, pl.ds(ys[1], h), pl.ds(xs[1], w)],
            send_sem=send_sem.at[sem], recv_sem=recv_sem.at[sem],
            device_id=device(dy, dx), device_id_type=MESH)

    flip(0)
    flip(1)
    pl.semaphore_wait(barrier, len(DIRS))
    first = [message((0, 2), dy, dx, k) for k, (dy, dx) in enumerate(DIRS)]
    for copy in first:
        copy.start()
    flip(RATE)
    rates = [message((RATE, 1), dy, dx, 28 + k, 1) for k, (dy, dx) in enumerate(DIRS) if not (dy and dx)]
    for copy in rates:
        copy.start()
    first += rates
    for slot in range(3, 5):
        flip(slot)
    later = [message((3, 1), dy, dx, 8 + k) for k, (dy, dx) in enumerate(DIRS)]
    for copy in later:
        copy.start()

    def local(n):
        rows_of(mobility, n, lo, 2, OWN, rows - 2)
        rows_of(chem, n, lo + 1, rows - 2, INNER)

    def before(n):
        rows_of(gflux, n, lo + 1, rows - 2, CORE)
        rows_of(update, n, lo + 2, rows - 4, MAIN)

    def rim(n):
        rows_of(mobility, n, lo - 2, 2, FULL, rows + 2)
        rows_of(chem, n, lo - 1, 4, FULL, 6)
        rows_of(chem, n, lo + 1, rows - 2, WIDE)

    def after(n):
        if n == 2:
            rows_of(gflux, n, lo - 1, 6, FULL, 4)
        else:
            rows_of(gflux, n, lo - 1, 4, FULL, 6)
        rows_of(gflux, n, lo + 1, rows - 2, WIDE)
        rows_of(update, n, lo, 4, OWN, 4)
        rows_of(update, n, lo + 2, rows - 4, EDGE)

    local(2)
    before(2)
    local(1)
    local(0)
    for copy in first:
        copy.wait_recv()
    rim(2)
    after(2)
    second = [message((5, 1), dy, dx, 16 + k) for k, (dy, dx) in enumerate(DIRS)]
    for copy in second:
        copy.start()
    late = [message((4, 1), dy, dx, 40 + k) for k, (dy, dx) in enumerate(DIRS)]
    for copy in late:
        copy.start()
    rows_of(grad, 2, lo, rows, ())
    for copy in later:
        copy.wait_recv()
    rim(1)
    before(1)
    rows_of(grad, 1, lo, rows, ())
    for copy in second:
        copy.wait_recv()
    after(1)
    third = [message((6, 1), dy, dx, 24 + k) for k, (dy, dx) in enumerate(DIRS)]
    for copy in third:
        copy.start()
    for copy in late:
        copy.wait_recv()
    rim(0)
    before(0)
    rows_of(grad, 0, lo, rows, ())
    for copy in third:
        copy.wait_recv()
    after(0)
    for copy in first + later + late + second + third:
        copy.wait_send()


def turn(rows, depth, new_ref, sum_ref, out_hbm, grad_hbm, outs, store_sem):
    stores = []
    for y in range(rows):
        outs[1, y] = new_ref[y].T
        s = sum_ref[y]
        outs[0, y] = (0.1 * (s + pltpu.roll(s, depth, 1))).T
        stores.append(pltpu.make_async_copy(outs.at[1, y], out_hbm.at[:, y, :], store_sem.at[1, y]))
        stores.append(pltpu.make_async_copy(outs.at[0, y, pl.ds(0, depth)], grad_hbm.at[:, y, :], store_sem.at[0, y]))
        for copy in stores[-2:]:
            copy.start()
    for copy in stores:
        copy.wait()


def solution(mesh):
    ngx, ngy = mesh.shape["gx"], mesh.shape["gy"]

    def shards(saved_conc, adjoint_end, rate_field):
        steps, frames, depth, rows, cols = saved_conc.shape
        lanes = frames * depth
        conc = saved_conc.reshape(steps, lanes, rows, cols)
        adj = adjoint_end.reshape(lanes, rows, cols)
        ext = (rows + 2 * HALO, cols + 2 * PAD, lanes)

        def kernel(*refs):
            body((ngx, ngy, rows, cols, depth), *refs)

        hbm = pl.BlockSpec(memory_space=pltpu.HBM)
        vmem = pl.BlockSpec(memory_space=pltpu.VMEM)
        tile = jax.ShapeDtypeStruct((rows, cols, lanes), jnp.float32)
        last, acc = pl.pallas_call(
            kernel,
            out_shape=(tile, tile),
            in_specs=[hbm] * 3, out_specs=(vmem, vmem),
            scratch_shapes=[
                pltpu.VMEM((5, rows, lanes, cols), jnp.float32),
                pltpu.VMEM((rows, depth, cols), jnp.float32),
                pltpu.VMEM((7, *ext), jnp.float32),
                pltpu.VMEM((3, *ext), jnp.float32),
                pltpu.VMEM((3, *ext), jnp.float32),
                pltpu.VMEM((3, *ext), jnp.float32),
                pltpu.VMEM(ext, jnp.float32),
                pltpu.VMEM(ext, jnp.float32),
                pltpu.SemaphoreType.DMA((5, rows)),
                pltpu.SemaphoreType.DMA((48,)),
                pltpu.SemaphoreType.DMA((48,)),
            ],
            compiler_params=pltpu.CompilerParams(
                collective_id=0, has_side_effects=True, vmem_limit_bytes=48 << 20),
        )(*(pltpu.with_memory_space_constraint(v, pltpu.HBM) for v in (conc, adj, rate_field)))
        out, grad = pl.pallas_call(
            functools.partial(turn, rows, depth),
            out_shape=(jax.ShapeDtypeStruct((lanes, rows, cols), jnp.float32),
                       jax.ShapeDtypeStruct((depth, rows, cols), jnp.float32)),
            in_specs=[vmem, vmem], out_specs=(hbm, hbm),
            scratch_shapes=[pltpu.VMEM((2, rows, lanes, cols), jnp.float32), pltpu.SemaphoreType.DMA((2, rows))],
            compiler_params=pltpu.CompilerParams(vmem_limit_bytes=8 << 20),
        )(last, acc)
        return out.reshape(adjoint_end.shape), grad

    return jax.shard_map(
        shards, mesh=mesh,
        in_specs=(P(None, None, None, "gy", "gx"), P(None, None, "gy", "gx"), P(None, "gy", "gx")),
        out_specs=(P(None, None, "gy", "gx"), P(None, "gy", "gx")),
        check_vma=False)
```

```python
import functools

import jax
import jax.numpy as jnp
from jax import lax
from jax.experimental import pallas as pl
from jax.experimental.pallas import tpu as pltpu
from jax.sharding import PartitionSpec as P

MESH = pl.DeviceIdType.MESH
DIRS = ((1, 1), (1, -1), (-1, 1), (-1, -1), (0, 1), (0, -1), (1, 0), (-1, 0))
ADJ, RATE, C, NEXT = 0, 2, (4, 3, 1), (0, 5, 6)
UNROLL = (4, 3, 2, 1)
HALO, PAD = 2, 16


def body(sizes, conc_hbm, adj_hbm, rate_hbm, last, turned,
         raw, raw_rate, acc, field, mob, pot, inv, gpot, part,
         load_sem, send_sem, recv_sem):
    ngx, ngy, rows, cols, depth = sizes
    gx, gy = lax.axis_index("gx"), lax.axis_index("gy")
    lo, hi = HALO, HALO + rows
    xl, xh = PAD, PAD + cols

    def device(dy, dx):
        return (lax.rem(gx + dx + ngx, ngx), lax.rem(gy + dy + ngy, ngy))

    barrier = pltpu.get_barrier_semaphore()
    for dy, dx in DIRS:
        pl.semaphore_signal(barrier, inc=1, device_id=device(dy, dx), device_id_type=MESH)

    loads = []
    for slot, src in enumerate((adj_hbm, conc_hbm.at[2], rate_hbm, conc_hbm.at[1], conc_hbm.at[0])):
        group = []
        for y in range(rows):
            dst = raw_rate.at[y] if slot == RATE else raw.at[slot, y]
            group.append(pltpu.make_async_copy(src.at[:, y, :], dst, load_sem.at[slot, y]))
            group[-1].start()
        loads.append(group)

    def flip(slot):
        for y in range(rows):
            loads[slot][y].wait()
            if slot == RATE:
                half = (0.1 * raw_rate[y]).T
                tile = jnp.concatenate([half, half], axis=-1)
            else:
                tile = raw[slot, y].T
            field[slot, lo + y, xl:xh, :] = tile

    lane = lax.broadcasted_iota(jnp.int32, (8, 128), 1)
    upper, lower = lax.rem(lane, depth) != depth - 1, lax.rem(lane, depth) != 0

    def pick(keep, v, other):
        return jnp.where(jnp.broadcast_to(keep[:1], v.shape), v, other)

    def up(v):
        return pltpu.roll(v, 127, 1)

    def down(v):
        return pltpu.roll(v, 1, 1)

    def laplace(ref, index, y, x, n):
        v = ref[(*index, y, pl.ds(x, n))]
        sides = (ref[(*index, y, pl.ds(x - 1, n))] + ref[(*index, y, pl.ds(x + 1, n))]
                 + ref[(*index, y - 1, pl.ds(x, n))] + ref[(*index, y + 1, pl.ds(x, n))])
        return v, sides - 6.0 * v + (pick(upper, up(v), v) + pick(lower, down(v), v))

    def mobility(n, y, pieces):
        for x, w in pieces:
            c = field[C[n], y, pl.ds(x, w)]
            mob[n, y, pl.ds(x, w)] = c * (1.0 - c)

    def chem(n, y, pieces):
        for x, w in pieces:
            c, lap = laplace(field, (C[n],), y, x, w)
            m = c * (1.0 - c)
            r = 1.0 / m
            mob[n, y, pl.ds(x, w)] = m
            inv[n, y, pl.ds(x, w)] = r
            pot[n, y, pl.ds(x, w)] = jnp.log(c * c * r) + 2.5 * (1.0 - 2.0 * c) - lap

    def gflux(n, y, pieces):
        src = NEXT[2 - n]
        for x, w in pieces:
            b, m, u = field[src, y, pl.ds(x, w)], mob[n, y, pl.ds(x, w)], pot[n, y, pl.ds(x, w)]
            step = pick(upper, up(b) - b, 0.0)
            flux = (up(m) + m) * step
            term = (up(u) - u) * step
            g, q = flux - down(flux), term + down(term)
            for dy, dx in ((0, 1), (0, -1), (1, 0), (-1, 0)):
                at = (y + dy, pl.ds(x + dx, w))
                d = field[(src, *at)] - b
                g = g + (mob[(n, *at)] + m) * d
                q = q + (pot[(n, *at)] - u) * d
            g = 0.015 * g - field[RATE, y, pl.ds(x, w)] * b
            gpot[y, pl.ds(x, w)] = g
            c = field[C[n], y, pl.ds(x, w)]
            part[y, pl.ds(x, w)] = b - (0.015 * (1.0 - 2.0 * c)) * q + (inv[n, y, pl.ds(x, w)] - 5.0) * g

    def update(n, y, pieces):
        for x, w in pieces:
            _, lap = laplace(gpot, (), y, x, w)
            new = part[y, pl.ds(x, w)] - lap
            if n == 0:
                last[y - lo, pl.ds(x - xl, w)] = new
            else:
                field[NEXT[3 - n], y, pl.ds(x, w)] = new

    def grad(n, y, _):
        for x in range(0, cols, 64):
            s = field[NEXT[2 - n], y, pl.ds(xl + x, 64)] * (0.5 - pot[n, y, pl.ds(xl + x, 64)])
            if n < 2:
                s = s + acc[y - lo, pl.ds(x, 64)]
            acc[y - lo, pl.ds(x, 64)] = s

    FULL = ((8, 144),)
    OWN = ((16, 128),)
    INNER = ((17, 64), (79, 64))
    CORE = ((18, 64), (78, 64))
    MAIN = ((24, 112),)
    WIDE = ((8, 16), (136, 16))
    EDGE = ((16, 8), (136, 8))

    def rows_of(fn, n, first, count, pieces, gap=0):
        step = next(u for u in UNROLL if count % u == 0)

        def some(k, _):
            for i in range(step):
                r = k * step + i
                fn(n, first + r + (gap * (r // (count // 2)) if gap else 0), pieces)
            return 0

        if step == count:
            some(0, 0)
        else:
            lax.fori_loop(0, count // step, some, 0)

    def message(fields, dy, dx, sem, ring=HALO):
        ring = 1 if dy and dx else ring
        ys = {1: (hi - ring, lo - ring), -1: (lo, hi), 0: (lo, lo)}[dy]
        xs = {1: (xh - ring, xl - ring), -1: (xl, xh), 0: (xl, xl)}[dx]
        h = ring if dy else rows
        w = ring if dx else cols
        f = pl.ds(*fields)
        return pltpu.make_async_remote_copy(
            src_ref=field.at[f, pl.ds(ys[0], h), pl.ds(xs[0], w)],
            dst_ref=field.at[f, pl.ds(ys[1], h), pl.ds(xs[1], w)],
            send_sem=send_sem.at[sem], recv_sem=recv_sem.at[sem],
            device_id=device(dy, dx), device_id_type=MESH)

    flip(0)
    flip(1)
    pl.semaphore_wait(barrier, len(DIRS))
    first = [message((0, 2), dy, dx, k) for k, (dy, dx) in enumerate(DIRS)]
    for copy in first:
        copy.start()
    flip(RATE)
    rates = [message((RATE, 1), dy, dx, 28 + k, 1) for k, (dy, dx) in enumerate(DIRS) if not (dy and dx)]
    for copy in rates:
        copy.start()
    first += rates
    for slot in range(3, 5):
        flip(slot)
    later = [message((3, 1), dy, dx, 8 + k) for k, (dy, dx) in enumerate(DIRS)]
    for copy in later:
        copy.start()

    def local(n):
        rows_of(mobility, n, lo, 2, OWN, rows - 2)
        rows_of(chem, n, lo + 1, rows - 2, INNER)

    def before(n):
        rows_of(gflux, n, lo + 1, rows - 2, CORE)
        rows_of(update, n, lo + 2, rows - 4, MAIN)

    def rim(n):
        rows_of(mobility, n, lo - 2, 2, FULL, rows + 2)
        rows_of(chem, n, lo - 1, 4, FULL, 6)
        rows_of(chem, n, lo + 1, rows - 2, WIDE)

    def after(n):
        if n == 2:
            rows_of(gflux, n, lo - 1, 6, FULL, 4)
        else:
            rows_of(gflux, n, lo - 1, 4, FULL, 6)
        rows_of(gflux, n, lo + 1, rows - 2, WIDE)
        rows_of(update, n, lo, 4, OWN, 4)
        rows_of(update, n, lo + 2, rows - 4, EDGE)

    local(2)
    before(2)
    for copy in first:
        copy.wait_recv()
    rim(2)
    after(2)
    second = [message((5, 1), dy, dx, 16 + k) for k, (dy, dx) in enumerate(DIRS)]
    for copy in second:
        copy.start()
    late = [message((4, 1), dy, dx, 40 + k) for k, (dy, dx) in enumerate(DIRS)]
    for copy in late:
        copy.start()
    rows_of(grad, 2, lo, rows, ())
    local(1)
    for copy in later:
        copy.wait_recv()
    rim(1)
    before(1)
    rows_of(grad, 1, lo, rows, ())
    for copy in second:
        copy.wait_recv()
    after(1)
    third = [message((6, 1), dy, dx, 24 + k) for k, (dy, dx) in enumerate(DIRS)]
    for copy in third:
        copy.start()
    local(0)
    for copy in late:
        copy.wait_recv()
    rim(0)
    before(0)
    rows_of(grad, 0, lo, rows, ())
    for y in range(rows):
        s = acc[y]
        turned[y] = (0.1 * (s + pltpu.roll(s, depth, 1))).T[:depth]
    for copy in third:
        copy.wait_recv()
    after(0)
    for copy in first + later + late + second + third:
        copy.wait_send()


def turn(rows, new_ref, grad_ref, out_hbm, grad_hbm, outs, store_sem):
    stores = []
    for y in range(rows):
        stores.append(pltpu.make_async_copy(grad_ref.at[y], grad_hbm.at[:, y, :], store_sem.at[0, y]))
        stores[-1].start()
    for y in range(rows):
        outs[y] = new_ref[y].T
        stores.append(pltpu.make_async_copy(outs.at[y], out_hbm.at[:, y, :], store_sem.at[1, y]))
        stores[-1].start()
    for copy in stores:
        copy.wait()


def solution(mesh):
    ngx, ngy = mesh.shape["gx"], mesh.shape["gy"]

    def shards(saved_conc, adjoint_end, rate_field):
        steps, frames, depth, rows, cols = saved_conc.shape
        lanes = frames * depth
        conc = saved_conc.reshape(steps, lanes, rows, cols)
        adj = adjoint_end.reshape(lanes, rows, cols)
        ext = (rows + 2 * HALO, cols + 2 * PAD, lanes)

        def kernel(*refs):
            body((ngx, ngy, rows, cols, depth), *refs)

        hbm = pl.BlockSpec(memory_space=pltpu.HBM)
        vmem = pl.BlockSpec(memory_space=pltpu.VMEM)
        last, grad = pl.pallas_call(
            kernel,
            out_shape=(jax.ShapeDtypeStruct((rows, cols, lanes), jnp.float32),
                       jax.ShapeDtypeStruct((rows, depth, cols), jnp.float32)),
            in_specs=[hbm] * 3, out_specs=(vmem, vmem),
            scratch_shapes=[
                pltpu.VMEM((5, rows, lanes, cols), jnp.float32),
                pltpu.VMEM((rows, depth, cols), jnp.float32),
                pltpu.VMEM((rows, cols, lanes), jnp.float32),
                pltpu.VMEM((7, *ext), jnp.float32),
                pltpu.VMEM((3, *ext), jnp.float32),
                pltpu.VMEM((3, *ext), jnp.float32),
                pltpu.VMEM((3, *ext), jnp.float32),
                pltpu.VMEM(ext, jnp.float32),
                pltpu.VMEM(ext, jnp.float32),
                pltpu.SemaphoreType.DMA((5, rows)),
                pltpu.SemaphoreType.DMA((48,)),
                pltpu.SemaphoreType.DMA((48,)),
            ],
            compiler_params=pltpu.CompilerParams(
                collective_id=0, has_side_effects=True, vmem_limit_bytes=48 << 20),
        )(*(pltpu.with_memory_space_constraint(v, pltpu.HBM) for v in (conc, adj, rate_field)))
        out, grad = pl.pallas_call(
            functools.partial(turn, rows),
            out_shape=(jax.ShapeDtypeStruct((lanes, rows, cols), jnp.float32),
                       jax.ShapeDtypeStruct((depth, rows, cols), jnp.float32)),
            in_specs=[vmem, vmem], out_specs=(hbm, hbm),
            scratch_shapes=[pltpu.VMEM((rows, lanes, cols), jnp.float32), pltpu.SemaphoreType.DMA((2, rows))],
            compiler_params=pltpu.CompilerParams(vmem_limit_bytes=8 << 20),
        )(last, grad)
        return out.reshape(adjoint_end.shape), grad

    return jax.shard_map(
        shards, mesh=mesh,
        in_specs=(P(None, None, None, "gy", "gx"), P(None, None, "gy", "gx"), P(None, "gy", "gx")),
        out_specs=(P(None, None, "gy", "gx"), P(None, "gy", "gx")),
        check_vma=False)
```

```python
import functools

import jax
import jax.numpy as jnp
from jax import lax
from jax.experimental import pallas as pl
from jax.experimental.pallas import tpu as pltpu
from jax.sharding import PartitionSpec as P

MESH = pl.DeviceIdType.MESH
DIRS = ((1, 1), (1, -1), (-1, 1), (-1, -1), (0, 1), (0, -1), (1, 0), (-1, 0))
ADJ, RATE, C, NEXT = 0, 2, (4, 3, 1), (0, 5, 6)
UNROLL = (4, 3, 2, 1)
HALO, PAD = 2, 16


def body(sizes, conc_hbm, adj_hbm, rate_hbm, last, turned,
         raw, raw_rate, acc, field, mob, pot, inv, gpot, part,
         load_sem, send_sem, recv_sem):
    ngx, ngy, rows, cols, depth = sizes
    gx, gy = lax.axis_index("gx"), lax.axis_index("gy")
    lo, hi = HALO, HALO + rows
    xl, xh = PAD, PAD + cols

    def device(dy, dx):
        return (lax.rem(gx + dx + ngx, ngx), lax.rem(gy + dy + ngy, ngy))

    barrier = pltpu.get_barrier_semaphore()
    for dy, dx in DIRS:
        pl.semaphore_signal(barrier, inc=1, device_id=device(dy, dx), device_id_type=MESH)

    loads = []
    for slot, src in enumerate((adj_hbm, conc_hbm.at[2], rate_hbm, conc_hbm.at[1], conc_hbm.at[0])):
        group = []
        for y in range(rows):
            dst = raw_rate.at[y] if slot == RATE else raw.at[slot, y]
            group.append(pltpu.make_async_copy(src.at[:, y, :], dst, load_sem.at[slot, y]))
            group[-1].start()
        loads.append(group)

    def flip(slot):
        for y in range(rows):
            loads[slot][y].wait()
            if slot == RATE:
                half = (0.1 * raw_rate[y]).T
                tile = jnp.concatenate([half, half], axis=-1)
            else:
                tile = raw[slot, y].T
            field[slot, lo + y, xl:xh, :] = tile

    lane = lax.broadcasted_iota(jnp.int32, (8, 128), 1)
    upper, lower = lax.rem(lane, depth) != depth - 1, lax.rem(lane, depth) != 0

    def pick(keep, v, other):
        return jnp.where(jnp.broadcast_to(keep[:1], v.shape), v, other)

    def up(v):
        return pltpu.roll(v, 127, 1)

    def down(v):
        return pltpu.roll(v, 1, 1)

    def laplace(ref, index, y, x, n):
        v = ref[(*index, y, pl.ds(x, n))]
        sides = (ref[(*index, y, pl.ds(x - 1, n))] + ref[(*index, y, pl.ds(x + 1, n))]
                 + ref[(*index, y - 1, pl.ds(x, n))] + ref[(*index, y + 1, pl.ds(x, n))])
        return v, sides - 6.0 * v + (pick(upper, up(v), v) + pick(lower, down(v), v))

    def mobility(n, y, pieces):
        for x, w in pieces:
            c = field[C[n], y, pl.ds(x, w)]
            mob[n, y, pl.ds(x, w)] = c * (1.0 - c)

    def chem(n, y, pieces):
        for x, w in pieces:
            c, lap = laplace(field, (C[n],), y, x, w)
            m = c * (1.0 - c)
            r = 1.0 / m
            mob[n, y, pl.ds(x, w)] = m
            inv[n, y, pl.ds(x, w)] = r
            pot[n, y, pl.ds(x, w)] = jnp.log(c * c * r) + 2.5 * (1.0 - 2.0 * c) - lap

    def gflux(n, y, pieces):
        src = NEXT[2 - n]
        for x, w in pieces:
            b, m, u = field[src, y, pl.ds(x, w)], mob[n, y, pl.ds(x, w)], pot[n, y, pl.ds(x, w)]
            step = pick(upper, up(b) - b, 0.0)
            flux = (up(m) + m) * step
            term = (up(u) - u) * step
            g, q = flux - down(flux), term + down(term)
            for dy, dx in ((0, 1), (0, -1), (1, 0), (-1, 0)):
                at = (y + dy, pl.ds(x + dx, w))
                d = field[(src, *at)] - b
                g = g + (mob[(n, *at)] + m) * d
                q = q + (pot[(n, *at)] - u) * d
            g = 0.015 * g - field[RATE, y, pl.ds(x, w)] * b
            gpot[y, pl.ds(x, w)] = g
            c = field[C[n], y, pl.ds(x, w)]
            part[y, pl.ds(x, w)] = b - (0.015 * (1.0 - 2.0 * c)) * q + (inv[n, y, pl.ds(x, w)] - 5.0) * g

    def update(n, y, pieces):
        for x, w in pieces:
            _, lap = laplace(gpot, (), y, x, w)
            new = part[y, pl.ds(x, w)] - lap
            if n == 0:
                last[y - lo, pl.ds(x - xl, w)] = new
            else:
                field[NEXT[3 - n], y, pl.ds(x, w)] = new

    def grad(n, y, _):
        for x in range(0, cols, 64):
            s = field[NEXT[2 - n], y, pl.ds(xl + x, 64)] * (0.5 - pot[n, y, pl.ds(xl + x, 64)])
            if n < 2:
                s = s + acc[y - lo, pl.ds(x, 64)]
            acc[y - lo, pl.ds(x, 64)] = s

    FULL = ((8, 144),)
    OWN = ((16, 128),)
    INNER = ((17, 64), (79, 64))
    CORE = ((18, 64), (78, 64))
    MAIN = ((24, 112),)
    WIDE = ((8, 16), (136, 16))
    EDGE = ((16, 8), (136, 8))

    def rows_of(fn, n, first, count, pieces, gap=0):
        step = next(u for u in UNROLL if count % u == 0)

        def some(k, _):
            for i in range(step):
                r = k * step + i
                fn(n, first + r + (gap * (r // (count // 2)) if gap else 0), pieces)
            return 0

        if step == count:
            some(0, 0)
        else:
            lax.fori_loop(0, count // step, some, 0)

    def message(fields, dy, dx, sem, ring=HALO):
        ring = 1 if dy and dx else ring
        ys = {1: (hi - ring, lo - ring), -1: (lo, hi), 0: (lo, lo)}[dy]
        xs = {1: (xh - ring, xl - ring), -1: (xl, xh), 0: (xl, xl)}[dx]
        h = ring if dy else rows
        w = ring if dx else cols
        f = pl.ds(*fields)
        return pltpu.make_async_remote_copy(
            src_ref=field.at[f, pl.ds(ys[0], h), pl.ds(xs[0], w)],
            dst_ref=field.at[f, pl.ds(ys[1], h), pl.ds(xs[1], w)],
            send_sem=send_sem.at[sem], recv_sem=recv_sem.at[sem],
            device_id=device(dy, dx), device_id_type=MESH)

    flip(0)
    flip(1)
    pl.semaphore_wait(barrier, len(DIRS))
    first = [message((0, 2), dy, dx, k) for k, (dy, dx) in enumerate(DIRS)]
    for copy in first:
        copy.start()
    flip(RATE)
    rates = [message((RATE, 1), dy, dx, 28 + k, 1) for k, (dy, dx) in enumerate(DIRS) if not (dy and dx)]
    for copy in rates:
        copy.start()
    first += rates
    for slot in range(3, 5):
        flip(slot)
    later = [message((3, 1), dy, dx, 8 + k) for k, (dy, dx) in enumerate(DIRS)]
    for copy in later:
        copy.start()

    def local(n):
        rows_of(mobility, n, lo, 2, OWN, rows - 2)
        rows_of(chem, n, lo + 1, rows - 2, INNER)

    def before(n):
        rows_of(gflux, n, lo + 1, rows - 2, CORE)
        rows_of(update, n, lo + 2, rows - 4, MAIN)

    def rim(n):
        rows_of(mobility, n, lo - 2, 2, FULL, rows + 2)
        rows_of(chem, n, lo - 1, 4, FULL, 6)
        rows_of(chem, n, lo + 1, rows - 2, WIDE)

    def after(n, corners=()):
        if n == 2:
            rows_of(gflux, n, lo - 1, 6, FULL, 4)
        else:
            rows_of(gflux, n, lo - 1, 4, FULL, 6)
            rows_of(gflux, n, lo + 1, rows - 2, WIDE)
        rows_of(update, n, lo, 2, OWN, rows - 2)
        for copy in corners:
            copy.start()
        if n == 2:
            rows_of(gflux, n, lo + 1, rows - 2, WIDE)
        rows_of(update, n, lo + 1, 2, OWN, rows - 4)
        rows_of(update, n, lo + 2, rows - 4, EDGE)

    local(2)
    before(2)
    for copy in first:
        copy.wait_recv()
    rim(2)
    second = [message((5, 1), dy, dx, 16 + k) for k, (dy, dx) in enumerate(DIRS)]
    after(2, second[:4])
    for copy in second[4:]:
        copy.start()
    late = [message((4, 1), dy, dx, 40 + k) for k, (dy, dx) in enumerate(DIRS)]
    for copy in late:
        copy.start()
    rows_of(grad, 2, lo, rows, ())
    local(1)
    for copy in later:
        copy.wait_recv()
    rim(1)
    before(1)
    rows_of(grad, 1, lo, rows, ())
    for copy in second:
        copy.wait_recv()
    third = [message((6, 1), dy, dx, 24 + k) for k, (dy, dx) in enumerate(DIRS)]
    after(1, third[:4])
    for copy in third[4:]:
        copy.start()
    local(0)
    for copy in late:
        copy.wait_recv()
    rim(0)
    before(0)
    rows_of(grad, 0, lo, rows, ())
    for y in range(rows):
        s = acc[y]
        turned[y] = (0.1 * (s + pltpu.roll(s, depth, 1))).T[:depth]
    for copy in third:
        copy.wait_recv()
    after(0)
    for copy in first + later + late + second + third:
        copy.wait_send()


def turn(rows, new_ref, grad_ref, out_hbm, grad_hbm, outs, store_sem):
    stores = []
    for y in range(rows):
        stores.append(pltpu.make_async_copy(grad_ref.at[y], grad_hbm.at[:, y, :], store_sem.at[0, y]))
        stores[-1].start()
    for y in range(rows):
        outs[y] = new_ref[y].T
        stores.append(pltpu.make_async_copy(outs.at[y], out_hbm.at[:, y, :], store_sem.at[1, y]))
        stores[-1].start()
    for copy in stores:
        copy.wait()


def solution(mesh):
    ngx, ngy = mesh.shape["gx"], mesh.shape["gy"]

    def shards(saved_conc, adjoint_end, rate_field):
        steps, frames, depth, rows, cols = saved_conc.shape
        lanes = frames * depth
        conc = saved_conc.reshape(steps, lanes, rows, cols)
        adj = adjoint_end.reshape(lanes, rows, cols)
        ext = (rows + 2 * HALO, cols + 2 * PAD, lanes)

        def kernel(*refs):
            body((ngx, ngy, rows, cols, depth), *refs)

        hbm = pl.BlockSpec(memory_space=pltpu.HBM)
        vmem = pl.BlockSpec(memory_space=pltpu.VMEM)
        last, grad = pl.pallas_call(
            kernel,
            out_shape=(jax.ShapeDtypeStruct((rows, cols, lanes), jnp.float32),
                       jax.ShapeDtypeStruct((rows, depth, cols), jnp.float32)),
            in_specs=[hbm] * 3, out_specs=(vmem, vmem),
            scratch_shapes=[
                pltpu.VMEM((5, rows, lanes, cols), jnp.float32),
                pltpu.VMEM((rows, depth, cols), jnp.float32),
                pltpu.VMEM((rows, cols, lanes), jnp.float32),
                pltpu.VMEM((7, *ext), jnp.float32),
                pltpu.VMEM((3, *ext), jnp.float32),
                pltpu.VMEM((3, *ext), jnp.float32),
                pltpu.VMEM((3, *ext), jnp.float32),
                pltpu.VMEM(ext, jnp.float32),
                pltpu.VMEM(ext, jnp.float32),
                pltpu.SemaphoreType.DMA((5, rows)),
                pltpu.SemaphoreType.DMA((48,)),
                pltpu.SemaphoreType.DMA((48,)),
            ],
            compiler_params=pltpu.CompilerParams(
                collective_id=0, has_side_effects=True, vmem_limit_bytes=48 << 20),
        )(*(pltpu.with_memory_space_constraint(v, pltpu.HBM) for v in (conc, adj, rate_field)))
        out, grad = pl.pallas_call(
            functools.partial(turn, rows),
            out_shape=(jax.ShapeDtypeStruct((lanes, rows, cols), jnp.float32),
                       jax.ShapeDtypeStruct((depth, rows, cols), jnp.float32)),
            in_specs=[vmem, vmem], out_specs=(hbm, hbm),
            scratch_shapes=[pltpu.VMEM((rows, lanes, cols), jnp.float32), pltpu.SemaphoreType.DMA((2, rows))],
            compiler_params=pltpu.CompilerParams(vmem_limit_bytes=8 << 20),
        )(last, grad)
        return out.reshape(adjoint_end.shape), grad

    return jax.shard_map(
        shards, mesh=mesh,
        in_specs=(P(None, None, None, "gy", "gx"), P(None, None, "gy", "gx"), P(None, "gy", "gx")),
        out_specs=(P(None, None, "gy", "gx"), P(None, "gy", "gx")),
        check_vma=False)
```
